512 devices in a mesh: row: 16 (over x_hi, y), col: 32 (over z, x_lo, core).
Axes of the slice: x: 4 (x_hi: 2, x_lo: 2; x = x_hi * 2 + x_lo), y: 8, z: 8, core: 2. Of those that a mesh axis runs over, the one named last changes fastest.
Arguments:
- amplitudes: bfloat16 [1024, 128, 1024], P('row', 'col'), may hold values from -3 to 3
- integrals: bfloat16 [3072, 131072], P('row', 'col'), may hold values from -0.015625 to 0.015625
- coefficients: bfloat16 [128, 1024, 3072], P('row', 'col'), may hold values from -0.109375 to 0.109375
Outputs:
- residual: bfloat16 [128, 1024, 1024], P('row', 'col')
The draws below stay inside these ranges and needn't reach their ends.
All inputs are finite; a program needn't handle non-finite values.
Results may differ from the reference program's by a relative error of at most 0.0066.
Values may be sent and summed in bfloat16 or wider, within the bound.
No kernel may reach another device: no remote copies, remote signals or barrier semaphores. Data moves between devices by JAX's collectives and lax.ppermute only.
A program may use at most 128 MiB of HBM per device.

```python
import jax
import jax.numpy as jnp
from jax import lax

O = 128
V = 1024
NAUX = 3072


def block_scale(key, extent, shards, low, high):
    def one(dim, parts):
        draws = jax.random.uniform(jax.random.fold_in(jax.random.fold_in(key, 6), dim), (parts,), jnp.float32, low / len(shards), high / len(shards))
        return jnp.repeat(jnp.exp(draws), extent[dim] // parts).reshape((-1,) + (1,) * (len(extent) - dim - 1))

    level = one(*shards[0])
    for cut in shards[1:]:
        level = level * one(*cut)
    return level


def noise(own_key, extent, width, bound, pieces=(), kind=jnp.bfloat16):
    gain = block_scale(own_key, extent, pieces, -0.22, 0.18) if pieces else 1.0
    values = jax.random.normal(own_key, extent, jnp.float32) * width * gain
    return jnp.minimum(jnp.maximum(values, -bound), bound).astype(kind)


def setup_inputs(seed: int = 0) -> dict:
    splits = jax.random.split(jax.random.key(seed), 4)
    return {
        "amplitudes": noise(splits[0], (V, O, V), 0.5, 3.0, ((0, 16), (1, 32))),
        "integrals": noise(splits[1], (NAUX, O * V), (O * V) ** -0.5, 0.015625, ((0, 16), (1, 32))),
        "coefficients": noise(splits[2], (O, V, NAUX), NAUX ** -0.5, 0.109375, ((0, 16), (1, 32))),
    }


def reference(amplitudes, integrals, coefficients):
    widened = amplitudes.astype(jnp.float32)
    folded = (2.0 * widened - jnp.transpose(widened, (2, 1, 0))).astype(jnp.bfloat16)
    fitted = lax.dot_general(folded.reshape(V, O * V), integrals, (((1,), (1,)), ((), ())), preferred_element_type=jnp.float32)
    fitted_half = fitted.astype(jnp.bfloat16)
    expanded = lax.dot_general(coefficients.reshape(O * V, NAUX), fitted_half, (((1,), (1,)), ((), ())), preferred_element_type=jnp.float32)
    expanded = expanded.astype(jnp.bfloat16).reshape(O, V, V).astype(jnp.float32)
    return (2.0 * jnp.swapaxes(expanded, 1, 2) - expanded).astype(jnp.bfloat16)
```

```python
import functools

import jax
import jax.numpy as jnp
from jax import lax
from jax.experimental import pallas as pl
from jax.experimental.pallas import tpu as pltpu
from jax.sharding import Mesh, PartitionSpec as P

F32, BF16 = jnp.float32, jnp.bfloat16
PLANE = ("xh", "z", "xl")
NT = (((1,), (1,)), ((), ()))
NN = (((1,), (0,)), ((), ()))


def dot(x, y, dims=NN):
    return lax.dot_general(x, y, dims, preferred_element_type=F32)


def split_matrix():
    m = lax.broadcasted_iota(jnp.int32, (256, 256), 0)
    n = lax.broadcasted_iota(jnp.int32, (256, 256), 1)
    source = ((n // 64) % 2) * 128 + ((n // 32) % 2) * 64 + (n // 128) * 32 + n % 32
    return (m == source).astype(BF16)


def fit_kernel(core_ref, a_ref, b_ref, own_ref, send_ref, acc_ref):
    kk, xh = pl.program_id(0), pl.program_id(1)

    @pl.when((kk == 0) & (xh == 0))
    def _():
        acc_ref[...] = jnp.zeros_like(acc_ref)

    rows = a_ref[...].reshape(512, 1024)
    half = pl.ds(pl.multiple_of(xh * 512, 512), 512)
    acc_ref[...] -= dot(b_ref[:, half], rows)
    acc_ref[:, half] += 2.0 * dot(b_ref[...], rows, NT)

    @pl.when((kk == 1) & (xh == 1))
    def _():
        swap = core_ref[0] == 1
        matrix = split_matrix()
        for t in range(4):
            part = dot(acc_ref[:, t * 256:(t + 1) * 256].astype(BF16), matrix)
            low, high = part[:, :128], part[:, 128:]
            at = slice((t % 2) * 128, (t % 2) * 128 + 128)
            own_ref[t // 2, :, at] = jnp.where(swap, high, low).astype(BF16)
            send_ref[t // 2, :, at] = jnp.where(swap, low, high).astype(BF16)


def fit(core, gathered, integrals):
    part = jax.ShapeDtypeStruct((2, 384, 256), BF16)
    whole = pl.BlockSpec((2, 384, 256), lambda k, x, c: (0, 0, 0))
    return pl.pallas_call(
        fit_kernel,
        out_shape=(part, part),
        grid_spec=pltpu.PrefetchScalarGridSpec(
            num_scalar_prefetch=1,
            grid=(2, 2),
            in_specs=[
                pl.BlockSpec((8, None, None, 64, 1024), lambda k, x, c: (0, x, k, 0, 0)),
                pl.BlockSpec((384, 1024), lambda k, x, c: (0, k)),
            ],
            out_specs=(whole, whole),
            scratch_shapes=[pltpu.VMEM((384, 1024), F32)],
        ),
        cost_estimate=pl.CostEstimate(
            flops=4 * 384 * 2048 * 1024, bytes_accessed=7 * 2**20, transcendentals=0
        ),
        name="fit",
    )(core, gathered, integrals)


def expand_kernel(core_ref, f_ref, own_ref, other_ref, kept_ref, passed_ref, turned_ref, both_ref):
    core = core_ref[0]
    for source, target, place in ((own_ref, kept_ref, core), (other_ref, passed_ref, 1 - core)):
        total = None
        for xh in range(2):
            columns = f_ref[:, xh].reshape(1536, 256)
            term = dot(source[:, xh * 1536:(xh + 1) * 1536], columns)
            total = term if total is None else total + term
        total = total.astype(BF16).reshape(8, 32, 256)
        target[...] = total
        both_ref[:, place] = total
    eye = (
        lax.broadcasted_iota(jnp.int32, (256, 256), 0)
        == lax.broadcasted_iota(jnp.int32, (256, 256), 1)
    ).astype(BF16)
    for t in range(2):
        block = both_ref[t * 4:(t + 1) * 4].reshape(256, 256)
        turned_ref[:, t * 256:(t + 1) * 256] = dot(eye, block, NT).astype(BF16)


def expand(core, fitted, own, other):
    kept = jax.ShapeDtypeStruct((8, 32, 512), BF16)
    piece = pl.BlockSpec((8, 32, 256), lambda t, c: (0, 0, t))
    table = pl.BlockSpec((256, 3072), lambda t, c: (0, 0))
    return pl.pallas_call(
        expand_kernel,
        out_shape=(kept, kept, jax.ShapeDtypeStruct((512, 512), BF16)),
        grid_spec=pltpu.PrefetchScalarGridSpec(
            num_scalar_prefetch=1,
            grid=(2,),
            in_specs=[
                pl.BlockSpec((8, None, 2, 192, 256), lambda t, c: (0, t, 0, 0, 0)),
                table,
                table,
            ],
            out_specs=(piece, piece, pl.BlockSpec((256, 512), lambda t, c: (t, 0))),
            scratch_shapes=[pltpu.VMEM((8, 2, 32, 256), BF16)],
        ),
        cost_estimate=pl.CostEstimate(
            flops=2 * 512 * 3072 * 512, bytes_accessed=7 * 2**20, transcendentals=0
        ),
        name="expand",
    )(core, fitted, own, other)


def finish_kernel(core_ref, arrived_ref, kept_ref, passed_ref, out_ref):
    swap = core_ref[0] == 1
    matrix = split_matrix()
    left = lax.broadcasted_iota(jnp.int32, (32, 128), 1) < 64
    kept = kept_ref[...].reshape(256, 512)
    passed = passed_ref[...].reshape(256, 512)
    for t in range(4):
        at = slice(t * 128, (t + 1) * 128)
        low = jnp.where(swap, passed[:, at], kept[:, at])
        high = jnp.where(swap, kept[:, at], passed[:, at])
        local = dot(jnp.concatenate([low, high], axis=1), matrix, NT)
        for j in range(8):
            tile = slice((j // 2) * 128, (j // 2) * 128 + 128)
            for s in range(2):
                first = arrived_ref[4 * t + 2 * s, :, tile].astype(F32)
                second = arrived_ref[4 * t + 2 * s + 1, :, tile].astype(F32)
                if j % 2 == 0:
                    second = pltpu.roll(second, 64, 1)
                else:
                    first = pltpu.roll(first, 64, 1)
                mirrored = jnp.where(left, first, second)
                mine = local[j * 32:(j + 1) * 32, s * 128:(s + 1) * 128]
                at_out = slice(t * 256 + s * 128, t * 256 + (s + 1) * 128)
                out_ref[j, :, at_out] = (2.0 * mirrored - mine).astype(BF16)


def finish(core, arrived, kept, passed):
    vmem = pl.BlockSpec(memory_space=pltpu.VMEM)
    return pl.pallas_call(
        finish_kernel,
        out_shape=jax.ShapeDtypeStruct((8, 32, 1024), BF16),
        in_specs=[pl.BlockSpec(memory_space=pltpu.SMEM), vmem, vmem, vmem],
        out_specs=vmem,
        cost_estimate=pl.CostEstimate(
            flops=2 * 256 * 1024 * 256, bytes_accessed=3 * 2**19, transcendentals=0
        ),
        name="finish",
    )(core, arrived, kept, passed)


def local(amplitudes, integrals, coefficients):
    core = lax.axis_index("core").astype(jnp.int32).reshape(1)
    partner = [(0, 1), (1, 0)]

    amps = jnp.transpose(amplitudes, (1, 0, 2))
    amps = lax.all_to_all(amps, "xh", split_axis=0, concat_axis=0, tiled=True)
    amps, integrals, coefficients = lax.optimization_barrier((amps, integrals, coefficients))
    gathered = lax.all_gather(amps, "y", axis=0, tiled=True).reshape(8, 2, 2, 64, 1024)
    integrals = lax.all_to_all(integrals, "xh", split_axis=1, concat_axis=0, tiled=True)
    own_c = coefficients.reshape(256, 3072)
    other_c = lax.ppermute(own_c, "core", partner)

    own, send = fit(core, gathered, integrals)
    got = lax.ppermute(send, "core", partner)
    chip = (own.astype(F32) + got.astype(F32)).astype(BF16).reshape(32, 24, 256)
    parts = lax.all_to_all(chip, PLANE, split_axis=0, concat_axis=0, tiled=True)
    summed = jnp.sum(parts.astype(F32), axis=0).astype(BF16)
    spread = jnp.broadcast_to(summed[None], (32, 24, 256))
    fitted = lax.all_to_all(spread, PLANE, split_axis=0, concat_axis=0, tiled=True)
    fitted = lax.all_gather(fitted.reshape(2, 384, 256), "y", axis=0, tiled=True)

    kept, passed, turned = expand(core, fitted.reshape(8, 2, 2, 192, 256), own_c, other_c)
    passed = lax.ppermute(passed, "core", partner)
    arrived = lax.all_to_all(turned, ("z", "xl"), split_axis=0, concat_axis=0, tiled=True)
    return finish(core, arrived.reshape(16, 32, 512), kept, passed)


def solution(mesh):
    fine = Mesh(mesh.devices.reshape(2, 8, 8, 2, 2), ("xh", "y", "z", "xl", "core"))
    row, col = ("xh", "y"), ("z", "xl", "core")
    in_specs = (P(row, col, None), P(row, col), P(row, col, None))
    return jax.shard_map(
        local, mesh=fine, in_specs=in_specs, out_specs=P(row, col, None), check_vma=False
    )
```

```python
import functools

import jax
import jax.numpy as jnp
from jax import lax
from jax.experimental import pallas as pl
from jax.experimental.pallas import tpu as pltpu
from jax.sharding import Mesh, PartitionSpec as P

F32, BF16 = jnp.float32, jnp.bfloat16
PLANE = ("xh", "z", "xl")
NT = (((1,), (1,)), ((), ()))
NN = (((1,), (0,)), ((), ()))


def dot(x, y, dims=NN):
    return lax.dot_general(x, y, dims, preferred_element_type=F32)


def split_matrix():
    m = lax.broadcasted_iota(jnp.int32, (256, 256), 0)
    n = lax.broadcasted_iota(jnp.int32, (256, 256), 1)
    source = ((n // 64) % 2) * 128 + ((n // 32) % 2) * 64 + (n // 128) * 32 + n % 32
    return (m == source).astype(BF16)


def split_lanes(x):
    matrix = split_matrix()
    parts = [dot(x[:, t * 256:(t + 1) * 256], matrix).astype(BF16) for t in range(4)]
    return jnp.concatenate([p[:, :128] for p in parts] + [p[:, 128:] for p in parts], axis=1)


def ready_kernel(xh_ref, a_ref, own_ref, send_ref):
    first = xh_ref[0] == 0
    for k in range(2):
        low = split_lanes(a_ref[:, k, :])
        high = split_lanes(a_ref[:, k + 2, :])
        own_ref[k] = jnp.where(first, low, high)
        send_ref[k] = jnp.where(first, high, low)


def ready(xh, amplitudes):
    half = jax.ShapeDtypeStruct((2, 64, 1024), BF16)
    vmem = pl.BlockSpec(memory_space=pltpu.VMEM)
    return pl.pallas_call(
        ready_kernel,
        out_shape=(half, half),
        in_specs=[pl.BlockSpec(memory_space=pltpu.SMEM), vmem],
        out_specs=(vmem, vmem),
        cost_estimate=pl.CostEstimate(
            flops=2 * 256 * 1024 * 256, bytes_accessed=2**20, transcendentals=0
        ),
        name="ready",
    )(xh, amplitudes)


def order_kernel(b_ref, out_ref):
    out_ref[...] = split_lanes(b_ref[...])


def order(integrals):
    block = pl.BlockSpec((384, 1024), lambda k: (0, k))
    return pl.pallas_call(
        order_kernel,
        out_shape=jax.ShapeDtypeStruct((384, 2048), BF16),
        grid=(2,),
        in_specs=[block],
        out_specs=block,
        cost_estimate=pl.CostEstimate(
            flops=2 * 384 * 2048 * 256, bytes_accessed=3 * 2**20, transcendentals=0
        ),
        name="order",
    )(integrals)


MOST = 104


def fit_kernel(where_ref, most_ref, rest_ref, b_ref, out_ref, acc_ref, rows_ref):
    step = pl.program_id(0)
    half, xh = where_ref[0], jnp.bitwise_xor(where_ref[1], step)

    @pl.when(step == 0)
    def _():
        acc_ref[...] = jnp.zeros_like(acc_ref)

    mine = pl.ds(pl.multiple_of(half * 512, 512), 512)
    place = pl.ds(pl.multiple_of(xh * 256, 256), 256)
    rows_ref[0] = most_ref[:, :64]
    rows_ref[1, :, :MOST - 64] = most_ref[:, 64:]
    rows_ref[1, :, MOST - 64:] = rest_ref[...]
    for k in range(2):
        for h in range(2):
            rows = rows_ref[k, :, h * 32:(h + 1) * 32, mine].reshape(256, 512)
            start = pl.multiple_of(k * 1024 + h * 512 + xh * 256, 256)
            acc_ref[...] -= dot(b_ref[:, pl.ds(start, 256)], rows)
        rows = rows_ref[k, :, pl.ds(pl.multiple_of(half * 32, 32), 32), :].reshape(256, 1024)
        acc_ref[:, place] += 2.0 * dot(b_ref[:, k * 1024:(k + 1) * 1024], rows, NT)

    @pl.when(step == 1)
    def _():
        for t in range(2):
            out_ref[t] = acc_ref[:, t * 256:(t + 1) * 256].astype(out_ref.dtype)


def fit(where, most, rest, integrals, dtype):
    return pl.pallas_call(
        fit_kernel,
        out_shape=jax.ShapeDtypeStruct((2, 384, 256), dtype),
        grid_spec=pltpu.PrefetchScalarGridSpec(
            num_scalar_prefetch=1,
            grid=(2,),
            in_specs=[
                pl.BlockSpec((8, None, MOST, 1024), lambda x, w: (0, x, 0, 0)),
                pl.BlockSpec((8, None, 128 - MOST, 1024), lambda x, w: (0, x, 0, 0)),
                pl.BlockSpec((384, 2048), lambda x, w: (0, 0)),
            ],
            out_specs=pl.BlockSpec((2, 384, 256), lambda x, w: (0, 0, 0)),
            scratch_shapes=[
                pltpu.VMEM((384, 512), F32),
                pltpu.VMEM((2, 8, 64, 1024), BF16),
            ],
        ),
        cost_estimate=pl.CostEstimate(
            flops=4 * 384 * 2048 * 512, bytes_accessed=6 * 2**20, transcendentals=0
        ),
        name="fit",
    )(where, most, rest, integrals)


def expand_kernel(core_ref, f_ref, own_ref, other_ref, kept_ref, passed_ref, turned_ref, both_ref):
    core = core_ref[0]
    for source, target, place in ((own_ref, kept_ref, core), (other_ref, passed_ref, 1 - core)):
        total = None
        for xh in range(2):
            columns = f_ref[:, xh].reshape(1536, 256)
            term = dot(source[:, xh * 1536:(xh + 1) * 1536], columns)
            total = term if total is None else total + term
        total = total.astype(BF16).reshape(8, 32, 256)
        target[...] = total
        both_ref[:, place] = total
    eye = (
        lax.broadcasted_iota(jnp.int32, (256, 256), 0)
        == lax.broadcasted_iota(jnp.int32, (256, 256), 1)
    ).astype(BF16)
    for t in range(2):
        block = both_ref[t * 4:(t + 1) * 4].reshape(256, 256)
        turned_ref[:, t * 256:(t + 1) * 256] = dot(eye, block, NT).astype(BF16)


def expand(core, fitted, own, other):
    kept = jax.ShapeDtypeStruct((8, 32, 512), BF16)
    piece = pl.BlockSpec((8, 32, 256), lambda t, c: (0, 0, t))
    table = pl.BlockSpec((256, 3072), lambda t, c: (0, 0))
    return pl.pallas_call(
        expand_kernel,
        out_shape=(kept, kept, jax.ShapeDtypeStruct((512, 512), BF16)),
        grid_spec=pltpu.PrefetchScalarGridSpec(
            num_scalar_prefetch=1,
            grid=(2,),
            in_specs=[
                pl.BlockSpec((8, None, 2, 192, 256), lambda t, c: (0, t, 0, 0, 0)),
                table,
                table,
            ],
            out_specs=(piece, piece, pl.BlockSpec((256, 512), lambda t, c: (t, 0))),
            scratch_shapes=[pltpu.VMEM((8, 2, 32, 256), BF16)],
        ),
        cost_estimate=pl.CostEstimate(
            flops=2 * 512 * 3072 * 512, bytes_accessed=7 * 2**20, transcendentals=0
        ),
        name="expand",
    )(core, fitted, own, other)


def finish_kernel(core_ref, arrived_ref, kept_ref, passed_ref, out_ref):
    swap = core_ref[0] == 1
    matrix = split_matrix()
    left = lax.broadcasted_iota(jnp.int32, (32, 128), 1) < 64
    kept = kept_ref[...].reshape(256, 512)
    passed = passed_ref[...].reshape(256, 512)
    for t in range(4):
        at = slice(t * 128, (t + 1) * 128)
        low = jnp.where(swap, passed[:, at], kept[:, at])
        high = jnp.where(swap, kept[:, at], passed[:, at])
        local = dot(jnp.concatenate([low, high], axis=1), matrix, NT)
        for j in range(8):
            tile = slice((j // 2) * 128, (j // 2) * 128 + 128)
            for s in range(2):
                first = arrived_ref[4 * t + 2 * s, :, tile].astype(F32)
                second = arrived_ref[4 * t + 2 * s + 1, :, tile].astype(F32)
                if j % 2 == 0:
                    second = pltpu.roll(second, 64, 1)
                else:
                    first = pltpu.roll(first, 64, 1)
                mirrored = jnp.where(left, first, second)
                mine = local[j * 32:(j + 1) * 32, s * 128:(s + 1) * 128]
                at_out = slice(t * 256 + s * 128, t * 256 + (s + 1) * 128)
                out_ref[j, :, at_out] = (2.0 * mirrored - mine).astype(BF16)


def finish(core, arrived, kept, passed):
    vmem = pl.BlockSpec(memory_space=pltpu.VMEM)
    return pl.pallas_call(
        finish_kernel,
        out_shape=jax.ShapeDtypeStruct((8, 32, 1024), BF16),
        in_specs=[pl.BlockSpec(memory_space=pltpu.SMEM), vmem, vmem, vmem],
        out_specs=vmem,
        cost_estimate=pl.CostEstimate(
            flops=2 * 256 * 1024 * 256, bytes_accessed=3 * 2**19, transcendentals=0
        ),
        name="finish",
    )(core, arrived, kept, passed)


def local(amplitudes, integrals, coefficients):
    core = lax.axis_index("core").astype(jnp.int32).reshape(1)
    xh = lax.axis_index("xh").astype(jnp.int32).reshape(1)
    partner = [(0, 1), (1, 0)]

    own, send = ready(xh, amplitudes)
    own, got = own.reshape(128, 1024), lax.ppermute(send, "xh", partner).reshape(128, 1024)
    most = jnp.concatenate([own[:MOST], got[:MOST]], axis=0)
    rest = jnp.concatenate([own[MOST:], got[MOST:]], axis=0)
    most, rest, integrals, coefficients = lax.optimization_barrier(
        (most, rest, integrals, coefficients)
    )
    most = lax.all_gather(most, "y", axis=0, tiled=True).reshape(8, 2, MOST, 1024)
    rest = lax.all_gather(rest, "y", axis=0, tiled=True).reshape(8, 2, 128 - MOST, 1024)
    integrals = lax.all_to_all(integrals, "xh", split_axis=1, concat_axis=0, tiled=True)
    integrals = order(integrals)
    own_c = coefficients.reshape(256, 3072)
    other_c = lax.ppermute(own_c, "core", partner)

    send = fit(jnp.concatenate([1 - core, xh]), most, rest, integrals, BF16)
    own = fit(jnp.concatenate([core, xh]), most, rest, integrals, F32)
    got = lax.ppermute(send, "core", partner)
    chip = (own + got.astype(F32)).astype(BF16).reshape(32, 24, 256)
    parts = lax.all_to_all(chip, PLANE, split_axis=0, concat_axis=0, tiled=True)
    summed = jnp.sum(parts.astype(F32), axis=0).astype(BF16)
    spread = jnp.broadcast_to(summed[None], (32, 24, 256))
    fitted = lax.all_to_all(spread, PLANE, split_axis=0, concat_axis=0, tiled=True)
    fitted = lax.all_gather(fitted.reshape(2, 384, 256), "y", axis=0, tiled=True)

    kept, passed, turned = expand(core, fitted.reshape(8, 2, 2, 192, 256), own_c, other_c)
    passed = lax.ppermute(passed, "core", partner)
    arrived = lax.all_to_all(turned, ("z", "xl"), split_axis=0, concat_axis=0, tiled=True)
    return finish(core, arrived.reshape(16, 32, 512), kept, passed)


def solution(mesh):
    fine = Mesh(mesh.devices.reshape(2, 8, 8, 2, 2), ("xh", "y", "z", "xl", "core"))
    row, col = ("xh", "y"), ("z", "xl", "core")
    in_specs = (P(row, col, None), P(row, col), P(row, col, None))
    return jax.shard_map(
        local, mesh=fine, in_specs=in_specs, out_specs=P(row, col, None), check_vma=False
    )
```

```python
import functools

import jax
import jax.numpy as jnp
from jax import lax
from jax.experimental import pallas as pl
from jax.experimental.pallas import tpu as pltpu
from jax.sharding import Mesh, PartitionSpec as P

F32, BF16 = jnp.float32, jnp.bfloat16
PLANE = ("xh", "z", "xl")
OFFSETS = (0, 1, -1, 2, -2, 3, -3, 4)


def device(xh, y, z, xl, core):
    return (((xh * 8 + y) * 8 + z) * 2 + xl) * 2 + core


def rings():
    near, far = ([], []), ([], [])
    for way, step in enumerate((1, -1)):
        for y in range(8):
            near[way].append((y * 2, (y + step) % 8 * 2))
            near[way].append((y * 2 + 1, (y - step) % 8 * 2 + 1))
            for z in range(8):
                at = (y * 8 + z) * 2
                far[way].append((at, ((y + step) % 8 * 8 + z) * 2))
                far[way].append((at + 1, (y * 8 + (z + step) % 8) * 2 + 1))
    return near, far


def planes():
    two, eight = range(2), range(8)
    groups = [[device(a, y, z, b, 0) for a in two for z in eight for b in two] for y in eight]
    return groups + [[device(a, y, z, b, 1) for a in two for y in eight for b in two] for z in eight]


def gather(starts, axes, pairs):
    ahead, back = list(starts), list(starts)
    blocks = [[x] for x in starts]
    for step in range(1, 5):
        for n in range(len(starts)):
            first, second = (ahead, back) if n % 2 == 0 else (back, ahead)
            way, other = (pairs[0], pairs[1]) if n % 2 == 0 else (pairs[1], pairs[0])
            first[n] = lax.ppermute(first[n], axes, way)
            blocks[n].append(first[n])
            if step < 4:
                second[n] = lax.ppermute(second[n], axes, other)
                blocks[n].append(second[n])
    return [block for ring in blocks for block in ring]
NT = (((1,), (1,)), ((), ()))
NN = (((1,), (0,)), ((), ()))


def dot(x, y, dims=NN):
    return lax.dot_general(x, y, dims, preferred_element_type=F32)


def split_matrix():
    m = lax.broadcasted_iota(jnp.int32, (256, 256), 0)
    n = lax.broadcasted_iota(jnp.int32, (256, 256), 1)
    source = ((n // 64) % 2) * 128 + ((n // 32) % 2) * 64 + (n // 128) * 32 + n % 32
    return (m == source).astype(BF16)


def fit_kernel(where_ref, *refs):
    blocks, (mine_ref, got_ref, own_ref, send_ref, rows_ref, table_ref, acc_ref, sems) = refs[:16], refs[16:]
    core, xh, y = where_ref[0], where_ref[1], where_ref[2]
    sign = 1 - 2 * core
    half = pl.ds(pl.multiple_of(xh * 2048, 2048), 2048)
    tables = [
        pltpu.make_async_copy(mine_ref.at[:, half], table_ref.at[xh], sems.at[0]),
        pltpu.make_async_copy(got_ref, table_ref.at[1 - xh], sems.at[1]),
    ]
    copies = ([], [])
    for k in range(2):
        for n, block in enumerate(blocks):
            side, offset = n // 8, OFFSETS[n % 8] if n < 8 else -OFFSETS[n % 8]
            source = jnp.bitwise_and(y - sign * offset, 7)
            start = pl.multiple_of(jnp.bitwise_xor(xh, side) * 512 + source * 64, 64)
            copies[k].append(
                pltpu.make_async_copy(
                    block.at[k], rows_ref.at[k, pl.ds(start, 64)], sems.at[2 + 16 * k + n]
                )
            )
    for copy in [*tables, *copies[0], *copies[1]]:
        copy.start()
    for copy in tables:
        copy.wait()
    for k in range(2):
        for copy in copies[k]:
            copy.wait()
        table = table_ref[:, :, k * 1024:(k + 1) * 1024].reshape(384, 1024)
        term = 2.0 * dot(table, rows_ref[k], NT) - dot(table, rows_ref[k])
        if k == 0:
            acc_ref[...] = term
        else:
            acc_ref[...] += term
    swap = core == 1
    matrix = split_matrix()
    for t in range(4):
        part = dot(acc_ref[:, t * 256:(t + 1) * 256].astype(BF16), matrix)
        low, high = part[:, :128], part[:, 128:]
        at = slice((t % 2) * 128, (t % 2) * 128 + 128)
        own_ref[t // 2, :, at] = jnp.where(swap, high, low).astype(BF16)
        send_ref[t // 2, :, at] = jnp.where(swap, low, high).astype(BF16)


def fit(where, blocks, mine, got):
    part = jax.ShapeDtypeStruct((2, 384, 256), BF16)
    whole = pl.BlockSpec((2, 384, 256), lambda i, w: (0, 0, 0))
    return pl.pallas_call(
        fit_kernel,
        out_shape=(part, part),
        grid_spec=pltpu.PrefetchScalarGridSpec(
            num_scalar_prefetch=1,
            grid=(1,),
            in_specs=[pl.BlockSpec(memory_space=pl.ANY)] * 18,
            out_specs=(whole, whole),
            scratch_shapes=[
                pltpu.VMEM((2, 1024, 1024), BF16),
                pltpu.VMEM((2, 192, 2048), BF16),
                pltpu.VMEM((384, 1024), F32),
                pltpu.SemaphoreType.DMA((34,)),
            ],
        ),
        cost_estimate=pl.CostEstimate(
            flops=4 * 384 * 2048 * 1024, bytes_accessed=7 * 2**20, transcendentals=0
        ),
        name="fit",
    )(where, *blocks, mine, got)


def expand_kernel(where_ref, *refs):
    blocks, rest = refs[:8], refs[8:]
    own_ref, other_ref, kept_ref, passed_ref, turned_ref, both_ref, f_ref, sems = rest
    core, spot, t = where_ref[0], where_ref[1], pl.program_id(0)

    def along_y(piece):
        for n, block in enumerate(blocks):
            source = jnp.bitwise_and(spot - OFFSETS[n], 7)
            for xh in range(2):
                yield pltpu.make_async_copy(
                    block.at[piece, pl.ds(4 * xh, 4)],
                    f_ref.at[piece, xh, source],
                    sems.at[piece * 16 + 2 * n + xh],
                )

    def along_z(piece):
        for n, block in enumerate(blocks):
            source = jnp.bitwise_and(spot - OFFSETS[n], 7)
            yield pltpu.make_async_copy(
                block.at[piece],
                f_ref.at[piece, source // 4, :, jnp.bitwise_and(source, 3)],
                sems.at[piece * 16 + 2 * n],
            )

    for number, copies in enumerate((along_y, along_z)):
        @pl.when((t == 0) & (core == number))
        def _():
            for piece in range(2):
                for copy in copies(piece):
                    copy.start()

    for number, copies in enumerate((along_y, along_z)):
        for piece in range(2):
            @pl.when((t == piece) & (core == number))
            def _():
                for copy in copies(piece):
                    copy.wait()

    for source, target, place in ((own_ref, kept_ref, core), (other_ref, passed_ref, 1 - core)):
        total = None
        for xh in range(2):
            columns = f_ref[t, xh].reshape(1536, 256)
            term = dot(source[:, xh * 1536:(xh + 1) * 1536], columns)
            total = term if total is None else total + term
        total = total.astype(BF16).reshape(8, 32, 256)
        target[...] = total
        both_ref[:, place] = total
    eye = (
        lax.broadcasted_iota(jnp.int32, (256, 256), 0)
        == lax.broadcasted_iota(jnp.int32, (256, 256), 1)
    ).astype(BF16)
    for h in range(2):
        block = both_ref[h * 4:(h + 1) * 4].reshape(256, 256)
        turned_ref[:, h * 256:(h + 1) * 256] = dot(eye, block, NT).astype(BF16)


def expand(where, blocks, own, other):
    kept = jax.ShapeDtypeStruct((8, 32, 512), BF16)
    piece = pl.BlockSpec((8, 32, 256), lambda t, w: (0, 0, t))
    table = pl.BlockSpec((256, 3072), lambda t, w: (0, 0))
    return pl.pallas_call(
        expand_kernel,
        out_shape=(kept, kept, jax.ShapeDtypeStruct((512, 512), BF16)),
        grid_spec=pltpu.PrefetchScalarGridSpec(
            num_scalar_prefetch=1,
            grid=(2,),
            in_specs=[pl.BlockSpec(memory_space=pl.ANY)] * 8 + [table, table],
            out_specs=(piece, piece, pl.BlockSpec((256, 512), lambda t, w: (t, 0))),
            scratch_shapes=[
                pltpu.VMEM((8, 2, 32, 256), BF16),
                pltpu.VMEM((2, 2, 8, 4, 48, 256), BF16),
                pltpu.SemaphoreType.DMA((32,)),
            ],
        ),
        cost_estimate=pl.CostEstimate(
            flops=2 * 512 * 3072 * 512, bytes_accessed=7 * 2**20, transcendentals=0
        ),
        name="expand",
    )(where, *blocks, own, other)


def finish_kernel(core_ref, arrived_ref, kept_ref, passed_ref, out_ref):
    swap = core_ref[0] == 1
    matrix = split_matrix()
    left = lax.broadcasted_iota(jnp.int32, (32, 128), 1) < 64
    kept = kept_ref[...].reshape(256, 512)
    passed = passed_ref[...].reshape(256, 512)
    for t in range(4):
        at = slice(t * 128, (t + 1) * 128)
        low = jnp.where(swap, passed[:, at], kept[:, at])
        high = jnp.where(swap, kept[:, at], passed[:, at])
        local = dot(jnp.concatenate([low, high], axis=1), matrix, NT)
        for j in range(8):
            tile = slice((j // 2) * 128, (j // 2) * 128 + 128)
            for s in range(2):
                first = arrived_ref[4 * t + 2 * s, :, tile].astype(F32)
                second = arrived_ref[4 * t + 2 * s + 1, :, tile].astype(F32)
                if j % 2 == 0:
                    second = pltpu.roll(second, 64, 1)
                else:
                    first = pltpu.roll(first, 64, 1)
                mirrored = jnp.where(left, first, second)
                mine = local[j * 32:(j + 1) * 32, s * 128:(s + 1) * 128]
                at_out = slice(t * 256 + s * 128, t * 256 + (s + 1) * 128)
                out_ref[j, :, at_out] = (2.0 * mirrored - mine).astype(BF16)


def finish(core, arrived, kept, passed):
    vmem = pl.BlockSpec(memory_space=pltpu.VMEM)
    return pl.pallas_call(
        finish_kernel,
        out_shape=jax.ShapeDtypeStruct((8, 32, 1024), BF16),
        in_specs=[pl.BlockSpec(memory_space=pltpu.SMEM), vmem, vmem, vmem],
        out_specs=vmem,
        cost_estimate=pl.CostEstimate(
            flops=2 * 256 * 1024 * 256, bytes_accessed=3 * 2**19, transcendentals=0
        ),
        name="finish",
    )(core, arrived, kept, passed)


def local(amplitudes, integrals, coefficients):
    core, xh, y, z = (lax.axis_index(n).astype(jnp.int32) for n in ("core", "xh", "y", "z"))
    partner = [(0, 1), (1, 0)]
    near, far = rings()

    amps = jnp.transpose(amplitudes, (1, 0, 2))
    leaving = lax.dynamic_slice(amps, (2 * (1 - xh), 0, 0), (2, 64, 1024))
    staying = lax.dynamic_slice(amps, (2 * xh, 0, 0), (2, 64, 1024))
    got = lax.ppermute(leaving, "xh", partner)
    blocks = gather([staying, got], ("y", "core"), near)
    blocks[1], integrals, coefficients = lax.optimization_barrier(
        (blocks[1], integrals, coefficients)
    )
    lent = lax.dynamic_slice(integrals, (0, 2048 * (1 - xh)), (192, 2048))
    lent = lax.ppermute(lent, "xh", partner)

    own, send = fit(jnp.stack([core, xh, y]), blocks, integrals, lent)
    got = lax.ppermute(send, "core", partner)
    chip = (own.astype(F32) + got.astype(F32)).astype(BF16).reshape(32, 24, 256)
    parts = lax.all_to_all(chip, PLANE, split_axis=0, concat_axis=0, tiled=True)
    summed = jnp.sum(parts.astype(F32), axis=0).astype(BF16)
    spread = jnp.broadcast_to(summed[None], (32, 24, 256))
    everyone = ("xh", "y", "z", "xl", "core")
    fitted = lax.all_to_all(
        spread, everyone, split_axis=0, concat_axis=0, tiled=True, axis_index_groups=planes()
    )
    fitted, coefficients = lax.optimization_barrier((fitted, coefficients))
    blocks = gather([fitted.reshape(2, 8, 48, 256)], ("y", "z", "core"), far)
    own_c = coefficients.reshape(256, 3072)
    other_c = lax.ppermute(own_c, "core", partner)

    where = jnp.stack([core, jnp.where(core == 0, y, z)])
    kept, passed, turned = expand(where, blocks, own_c, other_c)
    passed = lax.ppermute(passed, "core", partner)
    arrived = lax.all_to_all(turned, ("z", "xl"), split_axis=0, concat_axis=0, tiled=True)
    return finish(core.reshape(1), arrived.reshape(16, 32, 512), kept, passed)


def solution(mesh):
    fine = Mesh(mesh.devices.reshape(2, 8, 8, 2, 2), ("xh", "y", "z", "xl", "core"))
    row, col = ("xh", "y"), ("z", "xl", "core")
    in_specs = (P(row, col, None), P(row, col), P(row, col, None))
    return jax.shard_map(
        local, mesh=fine, in_specs=in_specs, out_specs=P(row, col, None), check_vma=False
    )
```

```python
import functools

import jax
import jax.numpy as jnp
from jax import lax
from jax.experimental import pallas as pl
from jax.experimental.pallas import tpu as pltpu
from jax.sharding import Mesh, PartitionSpec as P

F32, BF16 = jnp.float32, jnp.bfloat16
PLANE = ("xh", "z", "xl")
OFFSETS = (0, 1, -1, 2, -2, 3, -3, 4)


def device(xh, y, z, xl, core):
    return (((xh * 8 + y) * 8 + z) * 2 + xl) * 2 + core


def rings():
    near, far = ([], []), ([], [], [], [])
    for way, step in enumerate((1, -1, 2, -2)):
        for y in range(8):
            if way < 2:
                near[way].append((y * 2, (y + step) % 8 * 2))
                near[way].append((y * 2 + 1, (y - step) % 8 * 2 + 1))
            for z in range(8):
                at = (y * 8 + z) * 2
                far[way].append((at, ((y + step) % 8 * 8 + z) * 2))
                far[way].append((at + 1, (y * 8 + (z + step) % 8) * 2 + 1))
    return near, far


def planes():
    two, eight = range(2), range(8)
    groups = [[device(a, y, z, b, 0) for a in two for z in eight for b in two] for y in eight]
    return groups + [[device(a, y, z, b, 1) for a in two for y in eight for b in two] for z in eight]


def gather(starts, axes, pairs):
    ahead, back = list(starts), list(starts)
    blocks = [[x] for x in starts]
    for step in range(1, 5):
        for n in range(len(starts)):
            first, second = (ahead, back) if n % 2 == 0 else (back, ahead)
            way, other = (pairs[0], pairs[1]) if n % 2 == 0 else (pairs[1], pairs[0])
            first[n] = lax.ppermute(first[n], axes, way)
            blocks[n].append(first[n])
            if step < 4:
                second[n] = lax.ppermute(second[n], axes, other)
                blocks[n].append(second[n])
    return [block for ring in blocks for block in ring]
NT = (((1,), (1,)), ((), ()))
NN = (((1,), (0,)), ((), ()))


def dot(x, y, dims=NN):
    return lax.dot_general(x, y, dims, preferred_element_type=F32)


def split_matrix():
    m = lax.broadcasted_iota(jnp.int32, (256, 256), 0)
    n = lax.broadcasted_iota(jnp.int32, (256, 256), 1)
    source = ((n // 64) % 2) * 128 + ((n // 32) % 2) * 64 + (n // 128) * 32 + n % 32
    return (m == source).astype(BF16)


def fit_kernel(where_ref, *refs):
    blocks, (mine_ref, got_ref, own_ref, send_ref, rows_ref, table_ref, acc_ref, sems) = refs[:16], refs[16:]
    core, xh, y = where_ref[0], where_ref[1], where_ref[2]
    sign = 1 - 2 * core
    half = pl.ds(pl.multiple_of(xh * 2048, 2048), 2048)
    tables = [
        pltpu.make_async_copy(mine_ref.at[:, half], table_ref.at[xh], sems.at[0]),
        pltpu.make_async_copy(got_ref, table_ref.at[1 - xh], sems.at[1]),
    ]
    copies = ([], [])
    for k in range(2):
        for n, block in enumerate(blocks):
            side, offset = n // 8, OFFSETS[n % 8] if n < 8 else -OFFSETS[n % 8]
            source = jnp.bitwise_and(y - sign * offset, 7)
            start = pl.multiple_of(jnp.bitwise_xor(xh, side) * 512 + source * 64, 64)
            copies[k].append(
                pltpu.make_async_copy(
                    block.at[k], rows_ref.at[k, pl.ds(start, 64)], sems.at[2 + 16 * k + n]
                )
            )
    for copy in [*tables, *copies[0], *copies[1]]:
        copy.start()
    for copy in tables:
        copy.wait()
    for k in range(2):
        for copy in copies[k]:
            copy.wait()
        table = table_ref[:, :, k * 1024:(k + 1) * 1024].reshape(384, 1024)
        term = 2.0 * dot(table, rows_ref[k], NT) - dot(table, rows_ref[k])
        if k == 0:
            acc_ref[...] = term
        else:
            acc_ref[...] += term
    swap = core == 1
    matrix = split_matrix()
    for t in range(4):
        part = dot(acc_ref[:, t * 256:(t + 1) * 256].astype(BF16), matrix)
        low, high = part[:, :128], part[:, 128:]
        at = slice((t % 2) * 128, (t % 2) * 128 + 128)
        own_ref[t // 2, :, at] = jnp.where(swap, high, low).astype(BF16)
        send_ref[t // 2, :, at] = jnp.where(swap, low, high).astype(BF16)


def fit(where, blocks, mine, got):
    part = jax.ShapeDtypeStruct((2, 384, 256), BF16)
    whole = pl.BlockSpec((2, 384, 256), lambda i, w: (0, 0, 0))
    return pl.pallas_call(
        fit_kernel,
        out_shape=(part, part),
        grid_spec=pltpu.PrefetchScalarGridSpec(
            num_scalar_prefetch=1,
            grid=(1,),
            in_specs=[pl.BlockSpec(memory_space=pl.ANY)] * 18,
            out_specs=(whole, whole),
            scratch_shapes=[
                pltpu.VMEM((2, 1024, 1024), BF16),
                pltpu.VMEM((2, 192, 2048), BF16),
                pltpu.VMEM((384, 1024), F32),
                pltpu.SemaphoreType.DMA((34,)),
            ],
        ),
        cost_estimate=pl.CostEstimate(
            flops=4 * 384 * 2048 * 1024, bytes_accessed=7 * 2**20, transcendentals=0
        ),
        name="fit",
    )(where, *blocks, mine, got)


def expand_kernel(where_ref, *refs):
    blocks, rest = refs[:8], refs[8:]
    own_ref, other_ref, kept_ref, passed_ref, turned_ref, both_ref, f_ref, c_ref, sems = rest
    core, spot, t = where_ref[0], where_ref[1], pl.program_id(0)

    def along_y(piece):
        for n, block in enumerate(blocks):
            source = jnp.bitwise_and(spot - OFFSETS[n], 7)
            for xh in range(2):
                yield pltpu.make_async_copy(
                    block.at[piece, pl.ds(4 * xh, 4)],
                    f_ref.at[piece, xh, source],
                    sems.at[piece * 16 + 2 * n + xh],
                )

    def along_z(piece):
        for n, block in enumerate(blocks):
            source = jnp.bitwise_and(spot - OFFSETS[n], 7)
            yield pltpu.make_async_copy(
                block.at[piece],
                f_ref.at[piece, source // 4, :, jnp.bitwise_and(source, 3)],
                sems.at[piece * 16 + 2 * n],
            )

    tables = [
        pltpu.make_async_copy(own_ref, c_ref.at[core], sems.at[32]),
        pltpu.make_async_copy(other_ref, c_ref.at[1 - core], sems.at[33]),
    ]

    @pl.when(t == 0)
    def _():
        for copy in tables:
            copy.start()

    for number, copies in enumerate((along_y, along_z)):
        @pl.when((t == 0) & (core == number))
        def _():
            for piece in range(2):
                for copy in copies(piece):
                    copy.start()

    @pl.when(t == 0)
    def _():
        for copy in tables:
            copy.wait()

    for number, copies in enumerate((along_y, along_z)):
        for piece in range(2):
            @pl.when((t == piece) & (core == number))
            def _():
                for copy in copies(piece):
                    copy.wait()

    total = None
    for xh in range(2):
        columns = f_ref[t, xh].reshape(1536, 256)
        rows = c_ref[:, :, xh * 1536:(xh + 1) * 1536].reshape(512, 1536)
        term = dot(rows, columns)
        total = term if total is None else total + term
    total = total.astype(BF16)
    for c in range(2):
        both_ref[:, c] = total[c * 256:(c + 1) * 256].reshape(8, 32, 256)
    kept_ref[...] = both_ref[:, core]
    passed_ref[...] = both_ref[:, 1 - core]
    eye = (
        lax.broadcasted_iota(jnp.int32, (256, 256), 0)
        == lax.broadcasted_iota(jnp.int32, (256, 256), 1)
    ).astype(BF16)
    for h in range(2):
        block = both_ref[h * 4:(h + 1) * 4].reshape(256, 256)
        turned_ref[:, h * 256:(h + 1) * 256] = dot(eye, block, NT).astype(BF16)


def expand(where, blocks, own, other):
    kept = jax.ShapeDtypeStruct((8, 32, 512), BF16)
    piece = pl.BlockSpec((8, 32, 256), lambda t, w: (0, 0, t))
    return pl.pallas_call(
        expand_kernel,
        out_shape=(kept, kept, jax.ShapeDtypeStruct((512, 512), BF16)),
        grid_spec=pltpu.PrefetchScalarGridSpec(
            num_scalar_prefetch=1,
            grid=(2,),
            in_specs=[pl.BlockSpec(memory_space=pl.ANY)] * 10,
            out_specs=(piece, piece, pl.BlockSpec((256, 512), lambda t, w: (t, 0))),
            scratch_shapes=[
                pltpu.VMEM((8, 2, 32, 256), BF16),
                pltpu.VMEM((2, 2, 8, 4, 48, 256), BF16),
                pltpu.VMEM((2, 256, 3072), BF16),
                pltpu.SemaphoreType.DMA((34,)),
            ],
        ),
        cost_estimate=pl.CostEstimate(
            flops=2 * 512 * 3072 * 512, bytes_accessed=7 * 2**20, transcendentals=0
        ),
        name="expand",
    )(where, *blocks, own, other)


def finish_kernel(core_ref, arrived_ref, kept_ref, passed_ref, out_ref):
    swap = core_ref[0] == 1
    matrix = split_matrix()
    left = lax.broadcasted_iota(jnp.int32, (32, 128), 1) < 64
    kept = kept_ref[...].reshape(256, 512)
    passed = passed_ref[...].reshape(256, 512)
    for t in range(4):
        at = slice(t * 128, (t + 1) * 128)
        low = jnp.where(swap, passed[:, at], kept[:, at])
        high = jnp.where(swap, kept[:, at], passed[:, at])
        local = dot(jnp.concatenate([low, high], axis=1), matrix, NT)
        for j in range(8):
            tile = slice((j // 2) * 128, (j // 2) * 128 + 128)
            for s in range(2):
                first = arrived_ref[4 * t + 2 * s, :, tile].astype(F32)
                second = arrived_ref[4 * t + 2 * s + 1, :, tile].astype(F32)
                if j % 2 == 0:
                    second = pltpu.roll(second, 64, 1)
                else:
                    first = pltpu.roll(first, 64, 1)
                mirrored = jnp.where(left, first, second)
                mine = local[j * 32:(j + 1) * 32, s * 128:(s + 1) * 128]
                at_out = slice(t * 256 + s * 128, t * 256 + (s + 1) * 128)
                out_ref[j, :, at_out] = (2.0 * mirrored - mine).astype(BF16)


def finish(core, arrived, kept, passed):
    vmem = pl.BlockSpec(memory_space=pltpu.VMEM)
    return pl.pallas_call(
        finish_kernel,
        out_shape=jax.ShapeDtypeStruct((8, 32, 1024), BF16),
        in_specs=[pl.BlockSpec(memory_space=pltpu.SMEM), vmem, vmem, vmem],
        out_specs=vmem,
        cost_estimate=pl.CostEstimate(
            flops=2 * 256 * 1024 * 256, bytes_accessed=3 * 2**19, transcendentals=0
        ),
        name="finish",
    )(core, arrived, kept, passed)


def reach(own, axes, pairs):
    ahead, back, ahead_two, back_two = pairs
    one, minus_one = lax.ppermute(own, axes, ahead), lax.ppermute(own, axes, back)
    two, minus_two = lax.ppermute(own, axes, ahead_two), lax.ppermute(own, axes, back_two)
    three = lax.ppermute(one, axes, ahead_two)
    minus_three = lax.ppermute(minus_one, axes, back_two)
    four = lax.ppermute(three, axes, ahead)
    return [own, one, minus_one, two, minus_two, three, minus_three, four]


def local(amplitudes, integrals, coefficients):
    core, xh, y, z = (lax.axis_index(n).astype(jnp.int32) for n in ("core", "xh", "y", "z"))
    partner = [(0, 1), (1, 0)]
    near, far = rings()

    amps = jnp.transpose(amplitudes, (1, 0, 2))
    leaving = lax.dynamic_slice(amps, (2 * (1 - xh), 0, 0), (2, 64, 1024))
    staying = lax.dynamic_slice(amps, (2 * xh, 0, 0), (2, 64, 1024))
    got = lax.ppermute(leaving, "xh", partner)
    blocks = gather([staying, got], ("y", "core"), near)
    blocks[1], integrals = lax.optimization_barrier((blocks[1], integrals))
    blocks[7], coefficients = lax.optimization_barrier((blocks[7], coefficients))
    own_c = coefficients.reshape(256, 3072)
    other_c = lax.ppermute(own_c, "core", partner)
    lent = lax.dynamic_slice(integrals, (0, 2048 * (1 - xh)), (192, 2048))
    lent = lax.ppermute(lent, "xh", partner)

    own, send = fit(jnp.stack([core, xh, y]), blocks, integrals, lent)
    got = lax.ppermute(send, "core", partner)
    chip = (own.astype(F32) + got.astype(F32)).astype(BF16).reshape(32, 24, 256)
    parts = lax.all_to_all(chip, PLANE, split_axis=0, concat_axis=0, tiled=True)
    summed = jnp.sum(parts.astype(F32), axis=0).astype(BF16)
    spread = jnp.broadcast_to(summed[None], (32, 24, 256))
    everyone = ("xh", "y", "z", "xl", "core")
    fitted = lax.all_to_all(
        spread, everyone, split_axis=0, concat_axis=0, tiled=True, axis_index_groups=planes()
    )
    blocks = reach(fitted.reshape(2, 8, 48, 256), ("y", "z", "core"), far)

    where = jnp.stack([core, jnp.where(core == 0, y, z)])
    kept, passed, turned = expand(where, blocks, own_c, other_c)
    passed = lax.ppermute(passed, "core", partner)
    arrived = lax.all_to_all(turned, ("z", "xl"), split_axis=0, concat_axis=0, tiled=True)
    return finish(core.reshape(1), arrived.reshape(16, 32, 512), kept, passed)


def solution(mesh):
    fine = Mesh(mesh.devices.reshape(2, 8, 8, 2, 2), ("xh", "y", "z", "xl", "core"))
    row, col = ("xh", "y"), ("z", "xl", "core")
    in_specs = (P(row, col, None), P(row, col), P(row, col, None))
    return jax.shard_map(
        local, mesh=fine, in_specs=in_specs, out_specs=P(row, col, None), check_vma=False
    )
```

```python
import jax
import jax.numpy as jnp
from jax import lax
from jax.experimental import pallas as pl
from jax.experimental.pallas import tpu as pltpu
from jax.sharding import Mesh, PartitionSpec as P


F32, BF16 = jnp.float32, jnp.bfloat16
PLANE = ("xh", "z", "xl")
OFFSETS = (0, 1, -1, 2, -2, 3, -3, 4)


def device(xh, y, z, xl, core):
    return (((xh * 8 + y) * 8 + z) * 2 + xl) * 2 + core


def rings():
    near, far = ([], []), ([], [], [], [])
    for way, step in enumerate((1, -1, 2, -2)):
        for y in range(8):
            if way < 2:
                near[way].append((y * 2, (y + step) % 8 * 2))
                near[way].append((y * 2 + 1, (y - step) % 8 * 2 + 1))
            for z in range(8):
                at = (y * 8 + z) * 2
                far[way].append((at, ((y + step) % 8 * 8 + z) * 2))
                far[way].append((at + 1, (y * 8 + (z + step) % 8) * 2 + 1))
    return near, far


def planes():
    two, eight = range(2), range(8)
    groups = [[device(a, y, z, b, 0) for a in two for z in eight for b in two] for y in eight]
    return groups + [[device(a, y, z, b, 1) for a in two for y in eight for b in two] for z in eight]


def gather(starts, axes, pairs):
    moving = [[x, x] for x in starts]
    blocks = [[x] for x in starts]
    for step in range(1, 5):
        for n in range(len(starts)):
            for way in (0, 1) if n % 2 == 0 else (1, 0):
                if step < 4 or way == n % 2:
                    moving[n][way] = lax.ppermute(moving[n][way], axes, pairs[way])
                    blocks[n].append(moving[n][way])
    return [block for ring in blocks for block in ring]


NT = (((1,), (1,)), ((), ()))
NN = (((1,), (0,)), ((), ()))


def dot(x, y, dims=NN):
    return lax.dot_general(x, y, dims, preferred_element_type=F32)


def split_matrix():
    m = lax.broadcasted_iota(jnp.int32, (256, 256), 0)
    n = lax.broadcasted_iota(jnp.int32, (256, 256), 1)
    source = ((n // 64) % 2) * 128 + ((n // 32) % 2) * 64 + (n // 128) * 32 + n % 32
    return (m == source).astype(BF16)


def fit_kernel(where_ref, *refs):
    blocks, (mine_ref, got_ref, own_ref, send_ref, rows_ref, table_ref, sems) = refs[:16], refs[16:]
    core, xh, y = where_ref[0], where_ref[1], where_ref[2]
    sign = 1 - 2 * core
    half = pl.ds(pl.multiple_of(xh * 2048, 2048), 2048)
    tables = [
        pltpu.make_async_copy(mine_ref.at[:, half], table_ref.at[xh], sems.at[0]),
        pltpu.make_async_copy(got_ref, table_ref.at[1 - xh], sems.at[1]),
    ]
    copies = ([], [])
    for k in range(2):
        for n, block in enumerate(blocks):
            side, offset = n // 8, OFFSETS[n % 8] if n < 8 else -OFFSETS[n % 8]
            source = jnp.bitwise_and(y - sign * offset, 7)
            start = pl.multiple_of(jnp.bitwise_xor(xh, side) * 512 + source * 64, 64)
            copies[k].append(
                pltpu.make_async_copy(
                    block.at[k], rows_ref.at[k, pl.ds(start, 64)], sems.at[2 + 16 * k + n]
                )
            )
    for copy in [*tables, *copies[0], *copies[1]]:
        copy.start()
    for copy in tables:
        copy.wait()
    for copy in [*copies[0], *copies[1]]:
        copy.wait()
    swap = core == 1
    matrix = split_matrix()
    tables = [table_ref[:, :, k * 1024:(k + 1) * 1024].reshape(384, 1024) for k in range(2)]
    for t in range(4):
        at = slice(t * 256, (t + 1) * 256)
        direct = dot(tables[0], rows_ref[0, at], NT) + dot(tables[1], rows_ref[1, at], NT)
        mirrored = dot(tables[0], rows_ref[0, :, at]) + dot(tables[1], rows_ref[1, :, at])
        part = dot((2.0 * direct - mirrored).astype(BF16), matrix)
        low, high = part[:, :128], part[:, 128:]
        at = slice((t % 2) * 128, (t % 2) * 128 + 128)
        own_ref[t // 2, :, at] = jnp.where(swap, high, low).astype(BF16)
        send_ref[t // 2, :, at] = jnp.where(swap, low, high).astype(BF16)


def fit(where, blocks, mine, got):
    part = jax.ShapeDtypeStruct((2, 384, 256), BF16)
    whole = pl.BlockSpec((2, 384, 256), lambda i, w: (0, 0, 0))
    return pl.pallas_call(
        fit_kernel,
        out_shape=(part, part),
        grid_spec=pltpu.PrefetchScalarGridSpec(
            num_scalar_prefetch=1,
            grid=(1,),
            in_specs=[pl.BlockSpec(memory_space=pl.ANY)] * 18,
            out_specs=(whole, whole),
            scratch_shapes=[
                pltpu.VMEM((2, 1024, 1024), BF16),
                pltpu.VMEM((2, 192, 2048), BF16),
                pltpu.SemaphoreType.DMA((34,)),
            ],
        ),
        cost_estimate=pl.CostEstimate(
            flops=4 * 384 * 2048 * 1024, bytes_accessed=7 * 2**20, transcendentals=0
        ),
        name="fit",
    )(where, *blocks, mine, got)


def expand_kernel(where_ref, *refs):
    blocks, halves, rest = refs[:7], refs[7:9], refs[9:]
    own_ref, other_ref, kept_ref, passed_ref, turned_ref, both_ref, f_ref, c_ref, sems = rest
    core, spot, t = where_ref[0], where_ref[1], pl.program_id(0)

    def pieces(piece):
        for n, offset in enumerate(OFFSETS):
            block = blocks[n].at[piece] if n < 7 else halves[piece].at[0]
            yield n, jnp.bitwise_and(spot - offset, 7), block

    def along_y(piece):
        for n, source, block in pieces(piece):
            for xh in range(2):
                yield pltpu.make_async_copy(
                    block.at[pl.ds(4 * xh, 4)],
                    f_ref.at[piece, xh, source],
                    sems.at[piece * 16 + 2 * n + xh],
                )

    def along_z(piece):
        for n, source, block in pieces(piece):
            yield pltpu.make_async_copy(
                block,
                f_ref.at[piece, source // 4, :, jnp.bitwise_and(source, 3)],
                sems.at[piece * 16 + 2 * n],
            )

    tables = [
        pltpu.make_async_copy(own_ref, c_ref.at[core], sems.at[32]),
        pltpu.make_async_copy(other_ref, c_ref.at[1 - core], sems.at[33]),
    ]

    @pl.when(t == 0)
    def _():
        for copy in tables:
            copy.start()

    for number, copies in enumerate((along_y, along_z)):
        @pl.when((t == 0) & (core == number))
        def _():
            for piece in range(2):
                for copy in copies(piece):
                    copy.start()

    @pl.when(t == 0)
    def _():
        for copy in tables:
            copy.wait()

    for number, copies in enumerate((along_y, along_z)):
        for piece in range(2):
            @pl.when((t == piece) & (core == number))
            def _():
                for copy in copies(piece):
                    copy.wait()

    total = None
    for xh in range(2):
        columns = f_ref[t, xh].reshape(1536, 256)
        rows = c_ref[:, :, xh * 1536:(xh + 1) * 1536].reshape(512, 1536)
        term = dot(rows, columns)
        total = term if total is None else total + term
    total = total.astype(BF16)
    for c in range(2):
        both_ref[:, c] = total[c * 256:(c + 1) * 256].reshape(8, 32, 256)
    kept_ref[...] = both_ref[:, core]
    passed_ref[...] = both_ref[:, 1 - core]
    eye = (
        lax.broadcasted_iota(jnp.int32, (256, 256), 0)
        == lax.broadcasted_iota(jnp.int32, (256, 256), 1)
    ).astype(BF16)
    for h in range(2):
        block = both_ref[h * 4:(h + 1) * 4].reshape(256, 256)
        turned_ref[:, h * 256:(h + 1) * 256] = dot(eye, block, NT).astype(BF16)


def expand(where, blocks, own, other):
    kept = jax.ShapeDtypeStruct((8, 32, 512), BF16)
    piece = pl.BlockSpec((8, 32, 256), lambda t, w: (0, 0, t))
    return pl.pallas_call(
        expand_kernel,
        out_shape=(kept, kept, jax.ShapeDtypeStruct((512, 512), BF16)),
        grid_spec=pltpu.PrefetchScalarGridSpec(
            num_scalar_prefetch=1,
            grid=(2,),
            in_specs=[pl.BlockSpec(memory_space=pl.ANY)] * 11,
            out_specs=(piece, piece, pl.BlockSpec((256, 512), lambda t, w: (t, 0))),
            scratch_shapes=[
                pltpu.VMEM((8, 2, 32, 256), BF16),
                pltpu.VMEM((2, 2, 8, 4, 48, 256), BF16),
                pltpu.VMEM((2, 256, 3072), BF16),
                pltpu.SemaphoreType.DMA((34,)),
            ],
        ),
        cost_estimate=pl.CostEstimate(
            flops=2 * 512 * 3072 * 512, bytes_accessed=7 * 2**20, transcendentals=0
        ),
        name="expand",
    )(where, *blocks, own, other)


def finish_kernel(core_ref, arrived_ref, kept_ref, passed_ref, out_ref):
    swap = core_ref[0] == 1
    matrix = split_matrix()
    left = lax.broadcasted_iota(jnp.int32, (32, 128), 1) < 64
    kept = kept_ref[...].reshape(256, 512)
    passed = passed_ref[...].reshape(256, 512)
    for t in range(4):
        at = slice(t * 128, (t + 1) * 128)
        low = jnp.where(swap, passed[:, at], kept[:, at])
        high = jnp.where(swap, kept[:, at], passed[:, at])
        local = dot(jnp.concatenate([low, high], axis=1), matrix, NT)
        for j in range(8):
            tile = slice((j // 2) * 128, (j // 2) * 128 + 128)
            for s in range(2):
                first = arrived_ref[4 * t + 2 * s, :, tile].astype(F32)
                second = arrived_ref[4 * t + 2 * s + 1, :, tile].astype(F32)
                if j % 2 == 0:
                    second = pltpu.roll(second, 64, 1)
                else:
                    first = pltpu.roll(first, 64, 1)
                mirrored = jnp.where(left, first, second)
                mine = local[j * 32:(j + 1) * 32, s * 128:(s + 1) * 128]
                at_out = slice(t * 256 + s * 128, t * 256 + (s + 1) * 128)
                out_ref[j, :, at_out] = (2.0 * mirrored - mine).astype(BF16)


def finish(core, arrived, kept, passed):
    vmem = pl.BlockSpec(memory_space=pltpu.VMEM)
    return pl.pallas_call(
        finish_kernel,
        out_shape=jax.ShapeDtypeStruct((8, 32, 1024), BF16),
        in_specs=[pl.BlockSpec(memory_space=pltpu.SMEM), vmem, vmem, vmem],
        out_specs=vmem,
        cost_estimate=pl.CostEstimate(
            flops=2 * 256 * 1024 * 256, bytes_accessed=3 * 2**19, transcendentals=0
        ),
        name="finish",
    )(core, arrived, kept, passed)


def reach(own, axes, pairs):
    ahead, back, ahead_two, back_two = pairs
    one, minus_one = lax.ppermute(own, axes, ahead), lax.ppermute(own, axes, back)
    two, minus_two = lax.ppermute(own, axes, ahead_two), lax.ppermute(own, axes, back_two)
    three, minus_three = lax.ppermute(one, axes, ahead_two), lax.ppermute(minus_one, axes, back_two)
    four = lax.ppermute(two[:1], axes, ahead_two), lax.ppermute(minus_two[1:], axes, back_two)
    return [own, one, minus_one, two, minus_two, three, minus_three, *four]


def local(amplitudes, integrals, coefficients):
    core, xh, y, z = (lax.axis_index(n).astype(jnp.int32) for n in ("core", "xh", "y", "z"))
    partner = [(0, 1), (1, 0)]
    near, far = rings()

    amps = jnp.transpose(amplitudes, (1, 0, 2))
    leaving = lax.dynamic_slice(amps, (2 * (1 - xh), 0, 0), (2, 64, 1024))
    staying = lax.dynamic_slice(amps, (2 * xh, 0, 0), (2, 64, 1024))
    got = lax.ppermute(leaving, "xh", partner)
    blocks = gather([staying, got], ("y", "core"), near)
    blocks[1], integrals = lax.optimization_barrier((blocks[1], integrals))
    blocks[7], coefficients = lax.optimization_barrier((blocks[7], coefficients))
    own_c = coefficients.reshape(256, 3072)
    other_c = lax.ppermute(own_c, "core", partner)
    lent = lax.dynamic_slice(integrals, (0, 2048 * (1 - xh)), (192, 2048))
    lent = lax.ppermute(lent, "xh", partner)

    own, send = fit(jnp.stack([core, xh, y]), blocks, integrals, lent)
    got = lax.ppermute(send, "core", partner)
    chip = (own.astype(F32) + got.astype(F32)).astype(BF16).reshape(32, 24, 256)
    parts = lax.all_to_all(chip, PLANE, split_axis=0, concat_axis=0, tiled=True)
    summed = jnp.sum(parts.astype(F32), axis=0).astype(BF16)
    spread = jnp.broadcast_to(summed[None], (32, 24, 256))
    everyone = ("xh", "y", "z", "xl", "core")
    fitted = lax.all_to_all(
        spread, everyone, split_axis=0, concat_axis=0, tiled=True, axis_index_groups=planes()
    )
    blocks = reach(fitted.reshape(2, 8, 48, 256), ("y", "z", "core"), far)

    where = jnp.stack([core, jnp.where(core == 0, y, z)])
    kept, passed, turned = expand(where, blocks, own_c, other_c)
    passed = lax.ppermute(passed, "core", partner)
    arrived = lax.all_to_all(turned, ("z", "xl"), split_axis=0, concat_axis=0, tiled=True)
    return finish(core.reshape(1), arrived.reshape(16, 32, 512), kept, passed)


def solution(mesh):
    fine = Mesh(mesh.devices.reshape(2, 8, 8, 2, 2), ("xh", "y", "z", "xl", "core"))
    row, col = ("xh", "y"), ("z", "xl", "core")
    in_specs = (P(row, col, None), P(row, col), P(row, col, None))
    return jax.shard_map(
        local, mesh=fine, in_specs=in_specs, out_specs=P(row, col, None), check_vma=False
    )
```

```python
import jax
import jax.numpy as jnp
from jax import lax
from jax.experimental import pallas as pl
from jax.experimental.pallas import tpu as pltpu
from jax.sharding import Mesh, PartitionSpec as P


F32, BF16 = jnp.float32, jnp.bfloat16
PLANE = ("xh", "z", "xl")
OFFSETS = (0, 1, -1, 2, -2, 3, -3, 4)


def device(xh, y, z, xl, core):
    return (((xh * 8 + y) * 8 + z) * 2 + xl) * 2 + core


def rings():
    near, far = ([], []), ([], [], [], [])
    for way, step in enumerate((1, -1, 2, -2)):
        for y in range(8):
            if way < 2:
                near[way].append((y * 2, (y + step) % 8 * 2))
                near[way].append((y * 2 + 1, (y - step) % 8 * 2 + 1))
            for z in range(8):
                at = (y * 8 + z) * 2
                far[way].append((at, ((y + step) % 8 * 8 + z) * 2))
                far[way].append((at + 1, (y * 8 + (z + step) % 8) * 2 + 1))
    return near, far


def planes():
    two, eight = range(2), range(8)
    groups = [[device(a, y, z, b, 0) for a in two for z in eight for b in two] for y in eight]
    return groups + [[device(a, y, z, b, 1) for a in two for y in eight for b in two] for z in eight]


def gather(starts, axes, pairs):
    moving = [[x, x] for x in starts]
    blocks = [[x] for x in starts]
    for step in range(1, 5):
        for n in range(len(starts)):
            for way in (0, 1) if n % 2 == 0 else (1, 0):
                if step < 4 or way == n % 2:
                    moving[n][way] = lax.ppermute(moving[n][way], axes, pairs[way])
                    blocks[n].append(moving[n][way])
    return [block for ring in blocks for block in ring]


NT = (((1,), (1,)), ((), ()))
NN = (((1,), (0,)), ((), ()))


def dot(x, y, dims=NN):
    return lax.dot_general(x, y, dims, preferred_element_type=F32)


def split_matrix():
    m = lax.broadcasted_iota(jnp.int32, (256, 256), 0)
    n = lax.broadcasted_iota(jnp.int32, (256, 256), 1)
    source = ((n // 64) % 2) * 128 + ((n // 32) % 2) * 64 + (n // 128) * 32 + n % 32
    return (m == source).astype(BF16)


def fit_kernel(where_ref, *refs):
    blocks, (mine_ref, got_ref, own_ref, send_ref, rows_ref, table_ref, acc_ref, sems) = refs[:16], refs[16:]
    core, xh, y = where_ref[0], where_ref[1], where_ref[2]
    sign = 1 - 2 * core
    half = pl.ds(pl.multiple_of(xh * 2048, 2048), 2048)
    tables = [
        pltpu.make_async_copy(mine_ref.at[:, half], table_ref.at[xh], sems.at[0]),
        pltpu.make_async_copy(got_ref, table_ref.at[1 - xh], sems.at[1]),
    ]
    copies = ([], [])
    for k in range(2):
        for n, block in enumerate(blocks):
            side, offset = n // 8, OFFSETS[n % 8] if n < 8 else -OFFSETS[n % 8]
            source = jnp.bitwise_and(y - sign * offset, 7)
            start = pl.multiple_of(jnp.bitwise_xor(xh, side) * 512 + source * 64, 64)
            copies[k].append(
                pltpu.make_async_copy(
                    block.at[k], rows_ref.at[k, pl.ds(start, 64)], sems.at[2 + 16 * k + n]
                )
            )
    for copy in [*tables, *copies[0], *copies[1]]:
        copy.start()
    for copy in tables:
        copy.wait()
    for k in range(2):
        for copy in copies[k]:
            copy.wait()
        table = table_ref[:, :, k * 1024:(k + 1) * 1024].reshape(384, 1024)
        term = 2.0 * dot(table, rows_ref[k], NT) - dot(table, rows_ref[k])
        if k == 0:
            acc_ref[...] = term
        else:
            acc_ref[...] += term
    swap = core == 1
    matrix = split_matrix()
    for t in range(4):
        part = dot(acc_ref[:, t * 256:(t + 1) * 256].astype(BF16), matrix)
        low, high = part[:, :128], part[:, 128:]
        at = slice((t % 2) * 128, (t % 2) * 128 + 128)
        own_ref[t // 2, :, at] = jnp.where(swap, high, low).astype(BF16)
        send_ref[t // 2, :, at] = jnp.where(swap, low, high).astype(BF16)


def fit(where, blocks, mine, got):
    part = jax.ShapeDtypeStruct((2, 384, 256), BF16)
    whole = pl.BlockSpec((2, 384, 256), lambda i, w: (0, 0, 0))
    return pl.pallas_call(
        fit_kernel,
        out_shape=(part, part),
        grid_spec=pltpu.PrefetchScalarGridSpec(
            num_scalar_prefetch=1,
            grid=(1,),
            in_specs=[pl.BlockSpec(memory_space=pl.ANY)] * 18,
            out_specs=(whole, whole),
            scratch_shapes=[
                pltpu.VMEM((2, 1024, 1024), BF16),
                pltpu.VMEM((2, 192, 2048), BF16),
                pltpu.VMEM((384, 1024), F32),
                pltpu.SemaphoreType.DMA((34,)),
            ],
        ),
        cost_estimate=pl.CostEstimate(
            flops=4 * 384 * 2048 * 1024, bytes_accessed=7 * 2**20, transcendentals=0
        ),
        name="fit",
    )(where, *blocks, mine, got)


def expand_kernel(where_ref, *refs):
    blocks, rest = refs[:8], refs[8:]
    own_ref, other_ref, kept_ref, passed_ref, turned_ref, both_ref, f_ref, c_ref, sems = rest
    core, spot, t = where_ref[0], where_ref[1], pl.program_id(0)

    def along_y(piece):
        for n, block in enumerate(blocks):
            source = jnp.bitwise_and(spot - OFFSETS[n], 7)
            for xh in range(2):
                yield pltpu.make_async_copy(
                    block.at[piece, pl.ds(4 * xh, 4)],
                    f_ref.at[piece, xh, source],
                    sems.at[piece * 16 + 2 * n + xh],
                )

    def along_z(piece):
        for n, block in enumerate(blocks):
            source = jnp.bitwise_and(spot - OFFSETS[n], 7)
            yield pltpu.make_async_copy(
                block.at[piece],
                f_ref.at[piece, source // 4, :, jnp.bitwise_and(source, 3)],
                sems.at[piece * 16 + 2 * n],
            )

    tables = [
        pltpu.make_async_copy(own_ref, c_ref.at[core], sems.at[32]),
        pltpu.make_async_copy(other_ref, c_ref.at[1 - core], sems.at[33]),
    ]

    @pl.when(t == 0)
    def _():
        for copy in tables:
            copy.start()

    for number, copies in enumerate((along_y, along_z)):
        @pl.when((t == 0) & (core == number))
        def _():
            for piece in range(2):
                for copy in copies(piece):
                    copy.start()

    @pl.when(t == 0)
    def _():
        for copy in tables:
            copy.wait()

    for number, copies in enumerate((along_y, along_z)):
        for piece in range(2):
            @pl.when((t == piece) & (core == number))
            def _():
                for copy in copies(piece):
                    copy.wait()

    total = None
    for xh in range(2):
        columns = f_ref[t, xh].reshape(1536, 256)
        rows = c_ref[:, :, xh * 1536:(xh + 1) * 1536].reshape(512, 1536)
        term = dot(rows, columns)
        total = term if total is None else total + term
    total = total.astype(BF16)
    for c in range(2):
        both_ref[:, c] = total[c * 256:(c + 1) * 256].reshape(8, 32, 256)
    kept_ref[...] = both_ref[:, core]
    passed_ref[...] = both_ref[:, 1 - core]
    eye = (
        lax.broadcasted_iota(jnp.int32, (256, 256), 0)
        == lax.broadcasted_iota(jnp.int32, (256, 256), 1)
    ).astype(BF16)
    for h in range(2):
        block = both_ref[h * 4:(h + 1) * 4].reshape(256, 256)
        turned_ref[:, h * 256:(h + 1) * 256] = dot(eye, block, NT).astype(BF16)


def expand(where, blocks, own, other):
    kept = jax.ShapeDtypeStruct((8, 32, 512), BF16)
    piece = pl.BlockSpec((8, 32, 256), lambda t, w: (0, 0, t))
    return pl.pallas_call(
        expand_kernel,
        out_shape=(kept, kept, jax.ShapeDtypeStruct((512, 512), BF16)),
        grid_spec=pltpu.PrefetchScalarGridSpec(
            num_scalar_prefetch=1,
            grid=(2,),
            in_specs=[pl.BlockSpec(memory_space=pl.ANY)] * 10,
            out_specs=(piece, piece, pl.BlockSpec((256, 512), lambda t, w: (t, 0))),
            scratch_shapes=[
                pltpu.VMEM((8, 2, 32, 256), BF16),
                pltpu.VMEM((2, 2, 8, 4, 48, 256), BF16),
                pltpu.VMEM((2, 256, 3072), BF16),
                pltpu.SemaphoreType.DMA((34,)),
            ],
        ),
        cost_estimate=pl.CostEstimate(
            flops=2 * 512 * 3072 * 512, bytes_accessed=7 * 2**20, transcendentals=0
        ),
        name="expand",
    )(where, *blocks, own, other)


def finish_kernel(core_ref, arrived_ref, kept_ref, passed_ref, out_ref):
    swap = core_ref[0] == 1
    matrix = split_matrix()
    left = lax.broadcasted_iota(jnp.int32, (32, 128), 1) < 64
    kept = kept_ref[...].reshape(256, 512)
    passed = passed_ref[...].reshape(256, 512)
    for t in range(4):
        at = slice(t * 128, (t + 1) * 128)
        low = jnp.where(swap, passed[:, at], kept[:, at])
        high = jnp.where(swap, kept[:, at], passed[:, at])
        local = dot(jnp.concatenate([low, high], axis=1), matrix, NT)
        for j in range(8):
            tile = slice((j // 2) * 128, (j // 2) * 128 + 128)
            for s in range(2):
                first = arrived_ref[4 * t + 2 * s, :, tile].astype(F32)
                second = arrived_ref[4 * t + 2 * s + 1, :, tile].astype(F32)
                if j % 2 == 0:
                    second = pltpu.roll(second, 64, 1)
                else:
                    first = pltpu.roll(first, 64, 1)
                mirrored = jnp.where(left, first, second)
                mine = local[j * 32:(j + 1) * 32, s * 128:(s + 1) * 128]
                at_out = slice(t * 256 + s * 128, t * 256 + (s + 1) * 128)
                out_ref[j, :, at_out] = (2.0 * mirrored - mine).astype(BF16)


def finish(core, arrived, kept, passed):
    vmem = pl.BlockSpec(memory_space=pltpu.VMEM)
    return pl.pallas_call(
        finish_kernel,
        out_shape=jax.ShapeDtypeStruct((8, 32, 1024), BF16),
        in_specs=[pl.BlockSpec(memory_space=pltpu.SMEM), vmem, vmem, vmem],
        out_specs=vmem,
        cost_estimate=pl.CostEstimate(
            flops=2 * 256 * 1024 * 256, bytes_accessed=3 * 2**19, transcendentals=0
        ),
        name="finish",
    )(core, arrived, kept, passed)


def reach(own, axes, pairs):
    ahead, back, ahead_two, back_two = pairs
    one, minus_one = lax.ppermute(own, axes, ahead), lax.ppermute(own, axes, back)
    two, minus_two = lax.ppermute(own, axes, ahead_two), lax.ppermute(own, axes, back_two)
    three, minus_three = lax.ppermute(one, axes, ahead_two), lax.ppermute(minus_one, axes, back_two)
    four = lax.ppermute(two, axes, ahead_two)
    return [own, one, minus_one, two, minus_two, three, minus_three, four]


def local(amplitudes, integrals, coefficients):
    core, xh, y, z = (lax.axis_index(n).astype(jnp.int32) for n in ("core", "xh", "y", "z"))
    partner = [(0, 1), (1, 0)]
    near, far = rings()

    amps = jnp.transpose(amplitudes, (1, 0, 2))
    leaving = lax.dynamic_slice(amps, (2 * (1 - xh), 0, 0), (2, 64, 1024))
    staying = lax.dynamic_slice(amps, (2 * xh, 0, 0), (2, 64, 1024))
    got = lax.ppermute(leaving, "xh", partner)
    blocks = gather([staying, got], ("y", "core"), near)
    blocks[1], integrals = lax.optimization_barrier((blocks[1], integrals))
    own_c = coefficients.reshape(256, 3072)
    other_c = lax.ppermute(own_c, "core", partner)
    lent = lax.dynamic_slice(integrals, (0, 2048 * (1 - xh)), (192, 2048))
    lent = lax.ppermute(lent, "xh", partner)

    own, send = fit(jnp.stack([core, xh, y]), blocks, integrals, lent)
    got = lax.ppermute(send, "core", partner)
    chip = (own.astype(F32) + got.astype(F32)).astype(BF16).reshape(32, 24, 256)
    parts = lax.all_to_all(chip, PLANE, split_axis=0, concat_axis=0, tiled=True)
    summed = jnp.sum(parts.astype(F32), axis=0).astype(BF16)
    spread = jnp.broadcast_to(summed[None], (32, 24, 256))
    everyone = ("xh", "y", "z", "xl", "core")
    fitted = lax.all_to_all(
        spread, everyone, split_axis=0, concat_axis=0, tiled=True, axis_index_groups=planes()
    )
    blocks = reach(fitted.reshape(2, 8, 48, 256), ("y", "z", "core"), far)
    other_c, blocks[6] = lax.optimization_barrier((other_c, blocks[6]))

    where = jnp.stack([core, jnp.where(core == 0, y, z)])
    kept, passed, turned = expand(where, blocks, own_c, other_c)
    passed = lax.ppermute(passed, "core", partner)
    arrived = lax.all_to_all(turned, ("z", "xl"), split_axis=0, concat_axis=0, tiled=True)
    return finish(core.reshape(1), arrived.reshape(16, 32, 512), kept, passed)


def solution(mesh):
    fine = Mesh(mesh.devices.reshape(2, 8, 8, 2, 2), ("xh", "y", "z", "xl", "core"))
    row, col = ("xh", "y"), ("z", "xl", "core")
    in_specs = (P(row, col, None), P(row, col), P(row, col, None))
    return jax.shard_map(
        local, mesh=fine, in_specs=in_specs, out_specs=P(row, col, None), check_vma=False
    )
```
